32 devices in a mesh: pair: 8 (over z, core), cd: 4 (over y, x).
Axes of the slice: x: 2, y: 2, z: 4, core: 2. Of those that a mesh axis runs over, the one named last changes fastest.
Arguments:
- amplitudes: float32 [2048, 4096], P('pair', 'cd'), may hold values from -6 to 6
- integrals: float32 [4096, 256], P(('cd', 'pair')), may hold values from -0.09375 to 0.09375
- keep_tiles: int32 [32, 2], replicated, may hold values from 0 to 1, as said below
Outputs:
- ladder: float32 [2048, 256], P(('pair', 'cd'))
The draws below stay inside these ranges and needn't reach their ends.
Inputs may be any that keep to these rules, and one draw needn't show every extreme that they name: `keep_tiles`: each entry is 0 (tile screened out) or 1 (tile kept); each tile row keeps at most one tile, and some tile row keeps one.
All inputs are finite; a program needn't handle non-finite values.
Results may differ from the reference program's by a relative error of at most 0.000071.
Values sent between devices are 32-bit elements; how exact they have to be, the bound alone decides.
A program may use at most 64 MiB of HBM per device.

```python
import jax
import jax.numpy as jnp
from jax import lax

TILE = 128
AB = 256
CD = 4096
PAIRS = 2048


def draw_keep_tiles(key, part):
    rows_total = CD // TILE
    blocks = AB // TILE
    key_col = jax.random.fold_in(key, 11)
    key_live = jax.random.fold_in(key, 23)
    column = jax.random.randint(key_col, (rows_total,), 0, blocks)
    live = (jax.random.randint(key_live, (rows_total,), 0, 10) < 9).astype(jnp.int32)
    live = jnp.where(jnp.arange(rows_total) == 0, 1, live)
    onehot = (column[:, None] == jnp.arange(blocks)[None, :]).astype(jnp.int32)
    return onehot * live[:, None]


def block_levels(own_key, extent, pieces, low, high):
    def one(axis_at, shards_of):
        draws = jax.random.uniform(jax.random.fold_in(jax.random.fold_in(own_key, 6), axis_at), (shards_of,), jnp.float32, low / len(pieces), high / len(pieces))
        return jnp.repeat(jnp.exp(draws), extent[axis_at] // shards_of).reshape((-1,) + (1,) * (len(extent) - axis_at - 1))

    loudness = one(*pieces[0])
    for cut in pieces[1:]:
        loudness = loudness * one(*cut)
    return loudness


def noise(rng, extent, scale, most, pieces=(), dtype=jnp.bfloat16):
    gain = block_levels(rng, extent, pieces, -0.22, 0.18) if pieces else 1.0
    drawn = jax.random.normal(rng, extent, jnp.float32) * scale * gain
    return jnp.minimum(jnp.maximum(drawn, -most), most).astype(dtype)


def setup_inputs(seed: int = 0) -> dict:
    keys = jax.random.split(jax.random.key(seed), 4)
    amplitudes = noise(keys[0], (PAIRS, CD), 1.0, 6.0, ((0, 8), (1, 4)), jnp.float32)
    integrals = noise(keys[1], (CD, AB), CD ** -0.5, 0.09375, ((0, 32),), jnp.float32)
    keep_tiles = draw_keep_tiles(jax.random.fold_in(keys[3], 71), 0)
    return {"amplitudes": amplitudes, "integrals": integrals, "keep_tiles": keep_tiles}


def reference(amplitudes, integrals, keep_tiles):
    flags = keep_tiles.astype(jnp.float32)
    flags = jnp.repeat(jnp.repeat(flags, TILE, axis=0), TILE, axis=1)
    screened = integrals * flags
    return jnp.dot(amplitudes, screened, precision=lax.Precision.HIGHEST, preferred_element_type=jnp.float32)
```

```python
import functools

import jax
import jax.numpy as jnp
from jax import lax
from jax.experimental import pallas as pl
from jax.experimental.pallas import tpu as pltpu
from jax.sharding import PartitionSpec as P

TILE = 128
CORES = 2
HOLD = 1000
MESH = pl.DeviceIdType.MESH


def split(x):
    hi = x.astype(jnp.bfloat16)
    lo = (x - hi.astype(jnp.float32)).astype(jnp.bfloat16)
    return hi, lo


def kernel(pairs, cds, flags_hbm, v_hbm, a_hbm, out_ref, flags, v, a, tiles, a_cat, acc, land,
           load_sem, ssem, rsem, psend, precv, rs_send, rs_recv, zready, pready, cready, cgo):
    nz = pairs // CORES
    width = CORES * TILE
    me = lax.axis_index("pair")
    cd = lax.axis_index("cd")
    z = lax.div(me, CORES)
    core = lax.rem(me, CORES)
    partner = me + 1 - 2 * core
    blocks = v.shape[1] // TILE
    rows = out_ref.shape[0]

    load_v = pltpu.make_async_copy(v_hbm, v, load_sem.at[0])
    load_v.start()
    load_f = pltpu.make_async_copy(flags_hbm, flags, load_sem.at[2])
    load_f.start()
    load_a = pltpu.make_async_copy(a_hbm, a, load_sem.at[1])
    load_a.start()

    def signal(sem, axis, to):
        pl.semaphore_signal(sem, inc=1, device_id={axis: to}, device_id_type=MESH)

    barrier = pltpu.get_barrier_semaphore()
    for i in range(1, nz):
        @pl.when(z + i < nz)
        def _():
            signal(barrier, "pair", me + i * CORES)
    @pl.when(cd == 0)
    def _():
        for i in range(1, cds):
            signal(barrier, "cd", i)
    @pl.when(core == 1)
    def _():
        signal(barrier, "pair", partner)
    greeted = z + jnp.where(cd > 0, 1, 0) + 1 - core
    @pl.when(greeted > 0)
    def _():
        pl.semaphore_wait(barrier, greeted)
    for i in range(1, nz):
        @pl.when(z >= i)
        def _():
            signal(zready.at[z], "pair", me - i * CORES)
    @pl.when(core == 0)
    def _():
        signal(pready, "pair", partner)
    @pl.when(cd > 0)
    def _():
        signal(cready, "cd", 0)

    load_f.wait()
    load_v.wait()
    row_block = cd * pairs + me
    own = v[:, :TILE] * flags[0, row_block].astype(jnp.float32)
    for m in range(1, blocks):
        own = own + v[:, m * TILE:(m + 1) * TILE] * flags[m, row_block].astype(jnp.float32)
    tiles[me] = own.T

    def send(chip):
        return pltpu.make_async_remote_copy(
            src_ref=tiles.at[me], dst_ref=tiles.at[me], send_sem=ssem.at[chip], recv_sem=rsem.at[z],
            device_id={"pair": chip * CORES + core}, device_id_type=MESH)

    def arrival(chip):
        k = chip * CORES + core
        return pltpu.make_async_remote_copy(
            src_ref=tiles.at[k], dst_ref=tiles.at[k], send_sem=ssem.at[chip], recv_sem=rsem.at[chip],
            device_id={"pair": k}, device_id_type=MESH)

    def exchange(chip, side):
        k = chip * CORES + side
        return pltpu.make_async_remote_copy(
            src_ref=tiles.at[k], dst_ref=tiles.at[k], send_sem=psend.at[chip], recv_sem=precv.at[chip],
            device_id={"pair": partner}, device_id_type=MESH)

    @pl.when(z > 0)
    def _():
        send(0).start()
    @pl.when(core == 1)
    def _():
        pl.semaphore_wait(pready, 1)
    exchange(z, core).start()
    for i in range(1, nz):
        @pl.when(z + i < nz)
        def _():
            pl.semaphore_wait(zready.at[z + i], 1)
            send(z + i).start()
    exchange(z, 1 - core).wait_recv()
    @pl.when(z > 1)
    def _():
        pl.delay(HOLD)
    for i in range(1, nz - 1):
        @pl.when(z > i)
        def _():
            send(i).start()
    @pl.when(cd == 0)
    def _():
        pl.semaphore_wait(cready, cds - 1)
        for i in range(1, cds):
            signal(cgo, "cd", i)

    load_a.wait()
    hi, lo = split(a[...])
    for k in range(nz):
        c = slice(k * width, (k + 1) * width)
        a_cat[k] = jnp.concatenate([hi[:, c], lo[:, c], hi[:, c]], axis=1)

    def product(chip):
        stripes = []
        for i in range(CORES):
            k = chip * CORES + i
            t = tiles[k]
            g = cd * pairs + k
            stripes.append(jnp.concatenate(
                [t * flags[m, g].astype(jnp.float32) for m in range(blocks)], axis=0))
        b_hi, b_lo = split(jnp.concatenate(stripes, axis=1))
        return lax.dot_general(
            a_cat[chip], jnp.concatenate([b_hi, b_hi, b_lo], axis=1),
            dimension_numbers=(((1,), (1,)), ((), ())), preferred_element_type=jnp.float32)

    def source(j):
        return jnp.where(j <= z, z - j, j)

    def add(chip):
        exchange(chip, 1 - core).wait_recv()
        acc[...] += product(chip)

    acc[...] = product(z)

    def gather(j, carry):
        chip = source(j)
        arrival(chip).wait_recv()
        exchange(chip, core).start()
        @pl.when(core == 0)
        def _():
            add(chip)
        return carry

    def rest(j, carry):
        add(source(j))
        return carry

    lax.fori_loop(1, nz, gather, 0)
    @pl.when(core == 1)
    def _():
        lax.fori_loop(1, nz, rest, 0)

    def peer(j):
        return j + jnp.where(j >= cd, 1, 0)

    def scatter(j):
        q = peer(j)
        return pltpu.make_async_remote_copy(
            src_ref=acc.at[pl.ds(pl.multiple_of(q * rows, rows), rows)], dst_ref=land.at[cd],
            send_sem=rs_send.at[q], recv_sem=rs_recv.at[cd],
            device_id={"cd": q}, device_id_type=MESH)

    def landed(q):
        return pltpu.make_async_remote_copy(
            src_ref=acc.at[pl.ds(0, rows)], dst_ref=land.at[q], send_sem=rs_send.at[q], recv_sem=rs_recv.at[q],
            device_id={"cd": q}, device_id_type=MESH)

    @pl.when(cd > 0)
    def _():
        pl.semaphore_wait(cgo, 1)
    for j in range(cds - 1):
        scatter(j).start()

    def drain(j, carry):
        exchange(source(j), core).wait_send()
        send(source(j)).wait_send()
        return carry

    exchange(z, core).wait_send()
    lax.fori_loop(1, nz, drain, 0)

    total = acc[pl.ds(pl.multiple_of(cd * rows, rows), rows)]
    for j in range(cds - 1):
        q = peer(j)
        landed(q).wait_recv()
        total = total + land[q]
    out_ref[...] = total
    for j in range(cds - 1):
        scatter(j).wait_send()


def solution(mesh):
    pairs, cds = mesh.shape["pair"], mesh.shape["cd"]
    nz = pairs // CORES

    def local(amplitudes, integrals, keep_tiles):
        n, depth = amplitudes.shape
        ab = integrals.shape[1]
        rows = n // cds
        return pl.pallas_call(
            functools.partial(kernel, pairs, cds),
            out_shape=pltpu.VMEM((rows, ab), jnp.float32),
            in_specs=[
                pl.BlockSpec(memory_space=pl.ANY),
                pl.BlockSpec(memory_space=pl.ANY),
                pl.BlockSpec(memory_space=pl.ANY),
            ],
            out_specs=pl.BlockSpec(memory_space=pltpu.VMEM),
            scratch_shapes=[
                pltpu.SMEM(keep_tiles.shape[::-1], jnp.int32),
                pltpu.VMEM(integrals.shape, jnp.float32),
                pltpu.VMEM((n, depth), jnp.float32),
                pltpu.VMEM((pairs, TILE, TILE), jnp.float32),
                pltpu.VMEM((nz, n, 3 * CORES * TILE), jnp.bfloat16),
                pltpu.VMEM((n, ab), jnp.float32),
                pltpu.VMEM((cds, rows, ab), jnp.float32),
                pltpu.SemaphoreType.DMA((3,)),
                pltpu.SemaphoreType.DMA((nz,)),
                pltpu.SemaphoreType.DMA((nz,)),
                pltpu.SemaphoreType.DMA((nz,)),
                pltpu.SemaphoreType.DMA((nz,)),
                pltpu.SemaphoreType.DMA((cds,)),
                pltpu.SemaphoreType.DMA((cds,)),
                pltpu.SemaphoreType.REGULAR((nz,)),
                pltpu.SemaphoreType.REGULAR,
                pltpu.SemaphoreType.REGULAR,
                pltpu.SemaphoreType.REGULAR,
            ],
            compiler_params=pltpu.CompilerParams(collective_id=0, has_side_effects=True),
        )(keep_tiles.T, integrals, amplitudes)

    placed = (P("pair", "cd"), P(("cd", "pair"), None), P())
    return jax.shard_map(
        local, mesh=mesh, in_specs=placed, out_specs=P(("pair", "cd"), None), check_vma=False
    )
```

```python
import functools

import jax
import jax.numpy as jnp
from jax import lax
from jax.experimental import pallas as pl
from jax.experimental.pallas import tpu as pltpu
from jax.sharding import PartitionSpec as P

TILE = 128
CORES = 2
HOLDS = (1000, 700)
MESH = pl.DeviceIdType.MESH


def split(x):
    hi = x.astype(jnp.bfloat16)
    lo = (x - hi.astype(jnp.float32)).astype(jnp.bfloat16)
    return hi, lo


def kernel(pairs, cds, flags_hbm, v_hbm, a_hbm, out_ref, flags, v, a, tiles, a_cat, acc, land,
           load_sem, ssem, rsem, psend, precv, rs_send, rs_recv, zready, pready, cready, cgo, relay_sem):
    nz = pairs // CORES
    width = CORES * TILE
    me = lax.axis_index("pair")
    cd = lax.axis_index("cd")
    z = lax.div(me, CORES)
    core = lax.rem(me, CORES)
    partner = me + 1 - 2 * core
    blocks = v.shape[1] // TILE
    rows = out_ref.shape[0]

    load_v = pltpu.make_async_copy(v_hbm, v, load_sem.at[0])
    load_v.start()
    load_f = pltpu.make_async_copy(flags_hbm, flags, load_sem.at[2])
    load_f.start()
    load_a = pltpu.make_async_copy(a_hbm, a, load_sem.at[1])

    def signal(sem, axis, to):
        pl.semaphore_signal(sem, inc=1, device_id={axis: to}, device_id_type=MESH)

    barrier = pltpu.get_barrier_semaphore()
    for i in range(1, nz):
        @pl.when(z + i < nz)
        def _():
            signal(barrier, "pair", me + i * CORES)
    @pl.when(cd == 0)
    def _():
        for i in range(1, cds):
            signal(barrier, "cd", i)
    @pl.when(core == 1)
    def _():
        signal(barrier, "pair", partner)
    greeted = z + jnp.where(cd > 0, 1, 0) + 1 - core
    @pl.when(greeted > 0)
    def _():
        pl.semaphore_wait(barrier, greeted)
    for i in range(1, nz):
        @pl.when(z >= i)
        def _():
            signal(zready.at[z], "pair", me - i * CORES)
    @pl.when(core == 0)
    def _():
        signal(pready, "pair", partner)
    @pl.when(cd > 0)
    def _():
        signal(cready, "cd", 0)

    load_f.wait()
    load_v.wait()
    row_block = cd * pairs + me
    own = v[:, :TILE] * flags[0, row_block].astype(jnp.float32)
    for m in range(1, blocks):
        own = own + v[:, m * TILE:(m + 1) * TILE] * flags[m, row_block].astype(jnp.float32)
    tiles[me] = own

    def send(chip):
        return pltpu.make_async_remote_copy(
            src_ref=tiles.at[me], dst_ref=tiles.at[me], send_sem=ssem.at[chip], recv_sem=rsem.at[z],
            device_id={"pair": chip * CORES + core}, device_id_type=MESH)

    def arrival(chip):
        k = chip * CORES + core
        return pltpu.make_async_remote_copy(
            src_ref=tiles.at[k], dst_ref=tiles.at[k], send_sem=ssem.at[chip], recv_sem=rsem.at[chip],
            device_id={"pair": k}, device_id_type=MESH)

    def relay(to):
        k = 2 * CORES + 1
        return pltpu.make_async_remote_copy(
            src_ref=tiles.at[k], dst_ref=tiles.at[k], send_sem=relay_sem.at[to],
            recv_sem=rsem.at[2] if to else precv.at[2], device_id={"pair": to}, device_id_type=MESH)

    def exchange(chip, side):
        k = chip * CORES + side
        return pltpu.make_async_remote_copy(
            src_ref=tiles.at[k], dst_ref=tiles.at[k], send_sem=psend.at[chip], recv_sem=precv.at[chip],
            device_id={"pair": partner}, device_id_type=MESH)

    relayed = (z == 2) & (core == 1)
    @pl.when(relayed)
    def _():
        send(1).start()
    @pl.when((z > 0) & jnp.logical_not(relayed))
    def _():
        send(0).start()
    load_a.start()
    @pl.when(core == 1)
    def _():
        pl.semaphore_wait(pready, 1)
    exchange(z, core).start()
    for i in range(1, nz):
        @pl.when(z + i < nz)
        def _():
            pl.semaphore_wait(zready.at[z + i], 1)
            send(z + i).start()
    exchange(z, 1 - core).wait_recv()
    for side, hold in enumerate(HOLDS):
        @pl.when((z > 1) & (core == side) & jnp.logical_not(relayed))
        def _():
            pl.delay(hold)
            for i in range(1, nz - 1):
                @pl.when(z > i)
                def _():
                    send(i).start()
    @pl.when(cd == 0)
    def _():
        pl.semaphore_wait(cready, cds - 1)
        for i in range(1, cds):
            signal(cgo, "cd", i)

    load_a.wait()
    hi, lo = split(a[...])
    for k in range(nz):
        c = slice(k * width, (k + 1) * width)
        a_cat[k] = jnp.concatenate([hi[:, c], lo[:, c], hi[:, c]], axis=1)

    def product(chip):
        stripes = []
        for i in range(CORES):
            k = chip * CORES + i
            t = tiles[k]
            g = cd * pairs + k
            stripes.append(jnp.concatenate(
                [t * flags[m, g].astype(jnp.float32) for m in range(blocks)], axis=1))
        b_hi, b_lo = split(jnp.concatenate(stripes, axis=0))
        return lax.dot_general(
            a_cat[chip], jnp.concatenate([b_hi, b_hi, b_lo], axis=0),
            dimension_numbers=(((1,), (0,)), ((), ())), preferred_element_type=jnp.float32)

    def twice(chip):
        return (z == 0) & (core == 1) & (chip == 2)

    def source(j):
        chip = jnp.where(j <= z, z - j, j)
        if nz > 3:
            chip = jnp.where((z == 0) & (j == 2), 3, jnp.where((z == 0) & (j == 3), 2, chip))
        return chip

    def add(chip):
        exchange(chip, 1 - core).wait_recv()
        acc[...] += product(chip)

    acc[...] = product(z)

    def gather(j, carry):
        chip = source(j)
        receive(chip)
        @pl.when(core == 0)
        def _():
            add(chip)
        return carry

    def receive(chip):
        arrival(chip).wait_recv()
        @pl.when((z == 1) & (core == 1) & (chip == 2))
        def _():
            for i in range(CORES):
                relay(i).start()
        @pl.when(jnp.logical_not(twice(chip)))
        def _():
            exchange(chip, core).start()

    def rest(j, carry):
        add(source(j))
        return carry

    lax.fori_loop(1, nz - 1, gather, 0)
    last = source(nz - 1)
    receive(last)
    @pl.when(core == 1)
    def _():
        lax.fori_loop(1, nz - 1, rest, 0)

    def peer(j):
        return j + jnp.where(j >= cd, 1, 0)

    def scatter(q):
        return pltpu.make_async_remote_copy(
            src_ref=acc.at[pl.ds(q * rows, rows)], dst_ref=land.at[cd],
            send_sem=rs_send.at[q], recv_sem=rs_recv.at[cd],
            device_id={"cd": q}, device_id_type=MESH)

    def landed(q):
        return pltpu.make_async_remote_copy(
            src_ref=acc.at[pl.ds(0, rows)], dst_ref=land.at[q], send_sem=rs_send.at[q], recv_sem=rs_recv.at[q],
            device_id={"cd": q}, device_id_type=MESH)

    @pl.when(cd > 0)
    def _():
        pl.semaphore_wait(cgo, 1)
    exchange(last, 1 - core).wait_recv()
    prod = product(last)
    for q in range(cds):
        r = slice(q * rows, (q + 1) * rows)
        acc[r] += prod[r]
        @pl.when(cd != q)
        def _():
            scatter(q).start()

    def drain(j, carry):
        @pl.when(jnp.logical_not(twice(source(j))))
        def _():
            exchange(source(j), core).wait_send()
        @pl.when(jnp.logical_not(relayed & (source(j) == 0)))
        def _():
            send(source(j)).wait_send()
        return carry

    exchange(z, core).wait_send()
    lax.fori_loop(1, nz, drain, 0)
    @pl.when((z == 1) & (core == 1))
    def _():
        for i in range(CORES):
            relay(i).wait_send()

    total = acc[pl.ds(pl.multiple_of(cd * rows, rows), rows)]
    for j in range(cds - 1):
        q = peer(j)
        landed(q).wait_recv()
        total = total + land[q]
    out_ref[...] = total
    for j in range(cds - 1):
        landed(peer(j)).wait_send()


def solution(mesh):
    pairs, cds = mesh.shape["pair"], mesh.shape["cd"]
    nz = pairs // CORES

    def local(amplitudes, integrals, keep_tiles):
        n, depth = amplitudes.shape
        ab = integrals.shape[1]
        rows = n // cds
        return pl.pallas_call(
            functools.partial(kernel, pairs, cds),
            out_shape=pltpu.VMEM((rows, ab), jnp.float32),
            in_specs=[
                pl.BlockSpec(memory_space=pl.ANY),
                pl.BlockSpec(memory_space=pl.ANY),
                pl.BlockSpec(memory_space=pl.ANY),
            ],
            out_specs=pl.BlockSpec(memory_space=pltpu.VMEM),
            scratch_shapes=[
                pltpu.SMEM(keep_tiles.shape[::-1], jnp.int32),
                pltpu.VMEM(integrals.shape, jnp.float32),
                pltpu.VMEM((n, depth), jnp.float32),
                pltpu.VMEM((pairs, TILE, TILE), jnp.float32),
                pltpu.VMEM((nz, n, 3 * CORES * TILE), jnp.bfloat16),
                pltpu.VMEM((n, ab), jnp.float32),
                pltpu.VMEM((cds, rows, ab), jnp.float32),
                pltpu.SemaphoreType.DMA((3,)),
                pltpu.SemaphoreType.DMA((nz,)),
                pltpu.SemaphoreType.DMA((nz,)),
                pltpu.SemaphoreType.DMA((nz,)),
                pltpu.SemaphoreType.DMA((nz,)),
                pltpu.SemaphoreType.DMA((cds,)),
                pltpu.SemaphoreType.DMA((cds,)),
                pltpu.SemaphoreType.REGULAR((nz,)),
                pltpu.SemaphoreType.REGULAR,
                pltpu.SemaphoreType.REGULAR,
                pltpu.SemaphoreType.REGULAR,
                pltpu.SemaphoreType.DMA((CORES,)),
            ],
            compiler_params=pltpu.CompilerParams(collective_id=0, has_side_effects=True),
        )(keep_tiles.T, integrals, amplitudes)

    placed = (P("pair", "cd"), P(("cd", "pair"), None), P())
    return jax.shard_map(
        local, mesh=mesh, in_specs=placed, out_specs=P(("pair", "cd"), None), check_vma=False
    )
```

```python
import functools

import jax
import jax.numpy as jnp
from jax import lax
from jax.experimental import pallas as pl
from jax.experimental.pallas import tpu as pltpu
from jax.sharding import PartitionSpec as P

TILE = 128
CORES = 2
HOLDS = (1000, 700)
MESH = pl.DeviceIdType.MESH


def split(x):
    hi = x.astype(jnp.bfloat16)
    lo = (x - hi.astype(jnp.float32)).astype(jnp.bfloat16)
    return hi, lo


def kernel(pairs, cds, flags_hbm, v_hbm, a_hbm, out_ref, flags, v, a, tiles, a_cat, acc, land,
           load_sem, sent, rsem, precv, rs_send, rs_recv, zready, pready, entered, relay_sem):
    nz = pairs // CORES
    width = CORES * TILE
    me = lax.axis_index("pair")
    cd = lax.axis_index("cd")
    z = lax.div(me, CORES)
    core = lax.rem(me, CORES)
    partner = me + 1 - 2 * core
    blocks = v.shape[1] // TILE
    rows = out_ref.shape[0]

    load_v = pltpu.make_async_copy(v_hbm, v, load_sem.at[0])
    load_v.start()
    load_f = pltpu.make_async_copy(flags_hbm, flags, load_sem.at[2])
    load_f.start()
    load_a = pltpu.make_async_copy(a_hbm, a, load_sem.at[1])

    def signal(sem, axis, to):
        pl.semaphore_signal(sem, inc=1, device_id={axis: to}, device_id_type=MESH)

    barrier = pltpu.get_barrier_semaphore()
    for i in range(1, nz):
        @pl.when(z + i < nz)
        def _():
            signal(barrier, "pair", me + i * CORES)
    @pl.when(cd == 0)
    def _():
        for i in range(1, cds):
            signal(barrier, "cd", i)
    @pl.when(core == 1)
    def _():
        signal(barrier, "pair", partner)
    greeted = z + jnp.where(cd > 0, 1, 0) + 1 - core
    @pl.when(greeted > 0)
    def _():
        pl.semaphore_wait(barrier, greeted)
    for i in range(1, nz):
        @pl.when(z >= i)
        def _():
            signal(zready.at[i - 1], "pair", me - i * CORES)
    @pl.when(core == 0)
    def _():
        signal(pready, "pair", partner)
    @pl.when(cd > 0)
    def _():
        signal(entered, "cd", 0)

    load_f.wait()
    load_v.wait()
    row_block = cd * pairs + me
    own = v[:, :TILE] * flags[0, row_block].astype(jnp.float32)
    for m in range(1, blocks):
        own = own + v[:, m * TILE:(m + 1) * TILE] * flags[m, row_block].astype(jnp.float32)
    tiles[me] = own

    def send(chip):
        return pltpu.make_async_remote_copy(
            src_ref=tiles.at[me], dst_ref=tiles.at[me], send_sem=sent, recv_sem=rsem.at[z - jnp.where(z > chip, 1, 0)],
            device_id={"pair": chip * CORES + core}, device_id_type=MESH)

    def arrival(chip):
        k = chip * CORES + core
        return pltpu.make_async_remote_copy(
            src_ref=tiles.at[k], dst_ref=tiles.at[k], send_sem=sent, recv_sem=rsem.at[chip - jnp.where(chip > z, 1, 0)],
            device_id={"pair": k}, device_id_type=MESH)

    def relay(to):
        k = 2 * CORES + 1
        return pltpu.make_async_remote_copy(
            src_ref=tiles.at[k], dst_ref=tiles.at[k], send_sem=relay_sem,
            recv_sem=rsem.at[1] if to else precv.at[2], device_id={"pair": to}, device_id_type=MESH)

    def exchange(chip, side):
        k = chip * CORES + side
        return pltpu.make_async_remote_copy(
            src_ref=tiles.at[k], dst_ref=tiles.at[k], send_sem=sent, recv_sem=precv.at[chip],
            device_id={"pair": partner}, device_id_type=MESH)

    relayed = (z == 2) & (core == 1)
    @pl.when(relayed)
    def _():
        send(1).start()
    @pl.when((z > 0) & jnp.logical_not(relayed))
    def _():
        send(0).start()
    load_a.start()
    @pl.when(core == 1)
    def _():
        pl.semaphore_wait(pready, 1)
    exchange(z, core).start()
    for i in range(1, nz):
        @pl.when(z + i < nz)
        def _():
            pl.semaphore_wait(zready.at[i - 1], 1)
            send(z + i).start()
    exchange(z, 1 - core).wait_recv()
    for side, hold in enumerate(HOLDS):
        @pl.when((z > 1) & (core == side) & jnp.logical_not(relayed))
        def _():
            pl.delay(hold)
            for i in range(1, nz - 1):
                @pl.when(z > i)
                def _():
                    send(i).start()
    @pl.when(cd == 0)
    def _():
        pl.semaphore_wait(entered, cds - 1)
        for i in range(1, cds):
            signal(entered, "cd", i)

    load_a.wait()
    hi, lo = split(a[...])
    for k in range(nz):
        c = slice(k * width, (k + 1) * width)
        a_cat[k] = jnp.concatenate([hi[:, c], lo[:, c], hi[:, c]], axis=1)

    def product(chip):
        stripes = []
        for i in range(CORES):
            k = chip * CORES + i
            t = tiles[k]
            g = cd * pairs + k
            stripes.append(jnp.concatenate(
                [t * flags[m, g].astype(jnp.float32) for m in range(blocks)], axis=1))
        b_hi, b_lo = split(jnp.concatenate(stripes, axis=0))
        return lax.dot_general(
            a_cat[chip], jnp.concatenate([b_hi, b_hi, b_lo], axis=0),
            dimension_numbers=(((1,), (0,)), ((), ())), preferred_element_type=jnp.float32)

    def twice(chip):
        return (z == 0) & (core == 1) & (chip == 2)

    def source(j):
        chip = jnp.where(j <= z, z - j, j)
        if nz > 3:
            chip = jnp.where((z == 0) & (j == 2), 3, jnp.where((z == 0) & (j == 3), 2, chip))
        return chip

    def add(chip):
        exchange(chip, 1 - core).wait_recv()
        acc[...] += product(chip)

    acc[...] = product(z)

    def gather(j, carry):
        chip = source(j)
        receive(chip)
        @pl.when(core == 0)
        def _():
            add(chip)
        return carry

    def receive(chip):
        arrival(chip).wait_recv()
        @pl.when((z == 1) & (core == 1) & (chip == 2))
        def _():
            for i in range(CORES):
                relay(i).start()
        @pl.when(jnp.logical_not(twice(chip)))
        def _():
            exchange(chip, core).start()

    def rest(j, carry):
        add(source(j))
        return carry

    lax.fori_loop(1, nz - 1, gather, 0)
    last = source(nz - 1)
    receive(last)
    @pl.when(core == 1)
    def _():
        lax.fori_loop(1, nz - 1, rest, 0)

    def scatter(q):
        return pltpu.make_async_remote_copy(
            src_ref=acc.at[pl.ds(q * rows, rows)], dst_ref=land.at[cd - jnp.where(cd > q, 1, 0)],
            send_sem=rs_send, recv_sem=rs_recv, device_id={"cd": q}, device_id_type=MESH)

    def scattered():
        return pltpu.make_async_remote_copy(
            src_ref=acc.at[pl.ds(0, (cds - 1) * rows)], dst_ref=land,
            send_sem=rs_send, recv_sem=rs_recv, device_id={"cd": lax.rem(cd + 1, cds)}, device_id_type=MESH)

    @pl.when(cd > 0)
    def _():
        pl.semaphore_wait(entered, 1)
    exchange(last, 1 - core).wait_recv()
    prod = product(last)
    for q in range(cds):
        r = slice(q * rows, (q + 1) * rows)
        acc[r] += prod[r]
        @pl.when(cd != q)
        def _():
            scatter(q).start()

    def drained(n, sem):
        return pltpu.make_async_remote_copy(
            src_ref=tiles.at[pl.ds(0, n)], dst_ref=tiles.at[pl.ds(0, n)], send_sem=sem, recv_sem=rsem.at[0],
            device_id={"pair": partner}, device_id_type=MESH)

    fewer = relayed | twice(2)
    @pl.when(jnp.logical_not(fewer))
    def _():
        drained(2 * nz - 1, sent).wait_send()
    @pl.when(fewer)
    def _():
        drained(2 * nz - 2, sent).wait_send()
    @pl.when((z == 1) & (core == 1))
    def _():
        drained(CORES, relay_sem).wait_send()

    total = acc[pl.ds(pl.multiple_of(cd * rows, rows), rows)]
    scattered().wait_recv()
    for i in range(cds - 1):
        total = total + land[i]
    out_ref[...] = total
    scattered().wait_send()


def solution(mesh):
    pairs, cds = mesh.shape["pair"], mesh.shape["cd"]
    nz = pairs // CORES

    def local(amplitudes, integrals, keep_tiles):
        n, depth = amplitudes.shape
        ab = integrals.shape[1]
        rows = n // cds
        return pl.pallas_call(
            functools.partial(kernel, pairs, cds),
            out_shape=pltpu.VMEM((rows, ab), jnp.float32),
            in_specs=[
                pl.BlockSpec(memory_space=pl.ANY),
                pl.BlockSpec(memory_space=pl.ANY),
                pl.BlockSpec(memory_space=pl.ANY),
            ],
            out_specs=pl.BlockSpec(memory_space=pltpu.VMEM),
            scratch_shapes=[
                pltpu.SMEM(keep_tiles.shape[::-1], jnp.int32),
                pltpu.VMEM(integrals.shape, jnp.float32),
                pltpu.VMEM((n, depth), jnp.float32),
                pltpu.VMEM((pairs, TILE, TILE), jnp.float32),
                pltpu.VMEM((nz, n, 3 * CORES * TILE), jnp.bfloat16),
                pltpu.VMEM((n, ab), jnp.float32),
                pltpu.VMEM((cds - 1, rows, ab), jnp.float32),
                pltpu.SemaphoreType.DMA((3,)),
                pltpu.SemaphoreType.DMA,
                pltpu.SemaphoreType.DMA((nz - 1,)),
                pltpu.SemaphoreType.DMA((nz,)),
                pltpu.SemaphoreType.DMA,
                pltpu.SemaphoreType.DMA,
                pltpu.SemaphoreType.REGULAR((nz - 1,)),
                pltpu.SemaphoreType.REGULAR,
                pltpu.SemaphoreType.REGULAR,
                pltpu.SemaphoreType.DMA,
            ],
            compiler_params=pltpu.CompilerParams(collective_id=0, has_side_effects=True),
        )(keep_tiles.T, integrals, amplitudes)

    placed = (P("pair", "cd"), P(("cd", "pair"), None), P())
    return jax.shard_map(
        local, mesh=mesh, in_specs=placed, out_specs=P(("pair", "cd"), None), check_vma=False
    )
```

```python
import functools

import jax
import jax.numpy as jnp
from jax import lax
from jax.experimental import pallas as pl
from jax.experimental.pallas import tpu as pltpu
from jax.sharding import PartitionSpec as P

TILE = 128
CORES = 2
HOLDS = (1000, 700)
MESH = pl.DeviceIdType.MESH


def split(x):
    hi = x.astype(jnp.bfloat16)
    lo = (x - hi.astype(jnp.float32)).astype(jnp.bfloat16)
    return hi, lo


def kernel(pairs, cds, flags_hbm, v_hbm, a_hbm, out_ref, flags, v, a, tiles, a_cat, acc, land,
           sem, rsem, precv, rs_recv, zready, pready, entered):
    nz = pairs // CORES
    me = lax.axis_index("pair")
    cd = lax.axis_index("cd")
    z = lax.div(me, CORES)
    core = lax.rem(me, CORES)
    partner = me + 1 - 2 * core
    blocks = v.shape[1] // TILE
    rows = out_ref.shape[0]

    load_v = pltpu.make_async_copy(v_hbm, v, sem.at[0])
    load_v.start()
    load_f = pltpu.make_async_copy(flags_hbm, flags, sem.at[2])
    load_f.start()
    load_a = pltpu.make_async_copy(a_hbm, a, sem.at[1])

    def signal(sem, axis, to):
        pl.semaphore_signal(sem, inc=1, device_id={axis: to}, device_id_type=MESH)

    barrier = pltpu.get_barrier_semaphore()
    for i in range(1, nz):
        @pl.when(z + i < nz)
        def _():
            signal(barrier, "pair", me + i * CORES)
    @pl.when(cd == 0)
    def _():
        for i in range(1, cds):
            signal(barrier, "cd", i)
    @pl.when(core == 1)
    def _():
        signal(barrier, "pair", partner)
    greeted = z + jnp.where(cd > 0, 1, 0) + 1 - core
    @pl.when(greeted > 0)
    def _():
        pl.semaphore_wait(barrier, greeted)
    for i in range(1, nz):
        @pl.when(z >= i)
        def _():
            signal(zready.at[i - 1], "pair", me - i * CORES)
    @pl.when(core == 0)
    def _():
        signal(pready, "pair", partner)
    @pl.when(cd > 0)
    def _():
        signal(entered, "cd", 0)

    load_f.wait()
    load_v.wait()
    row_block = cd * pairs + me
    own = v[:, :TILE] * flags[0, row_block].astype(jnp.float32)
    for m in range(1, blocks):
        own = own + v[:, m * TILE:(m + 1) * TILE] * flags[m, row_block].astype(jnp.float32)
    tiles[me] = own

    def send(chip):
        return pltpu.make_async_remote_copy(
            src_ref=tiles.at[me], dst_ref=tiles.at[me], send_sem=sem.at[0], recv_sem=rsem.at[z - jnp.where(z > chip, 1, 0)],
            device_id={"pair": chip * CORES + core}, device_id_type=MESH)

    def arrival(chip):
        k = chip * CORES + core
        return pltpu.make_async_remote_copy(
            src_ref=tiles.at[k], dst_ref=tiles.at[k], send_sem=sem.at[0], recv_sem=rsem.at[chip - jnp.where(chip > z, 1, 0)],
            device_id={"pair": k}, device_id_type=MESH)

    def relay(to):
        k = 2 * CORES + 1
        return pltpu.make_async_remote_copy(
            src_ref=tiles.at[k], dst_ref=tiles.at[k], send_sem=sem.at[1],
            recv_sem=rsem.at[1] if to else precv.at[2], device_id={"pair": to}, device_id_type=MESH)

    def exchange(chip, side):
        k = chip * CORES + side
        return pltpu.make_async_remote_copy(
            src_ref=tiles.at[k], dst_ref=tiles.at[k], send_sem=sem.at[0], recv_sem=precv.at[chip],
            device_id={"pair": partner}, device_id_type=MESH)

    relayed = (z == 2) & (core == 1)
    @pl.when(relayed)
    def _():
        send(1).start()
    @pl.when((z > 0) & jnp.logical_not(relayed))
    def _():
        send(0).start()
    load_a.start()
    @pl.when(core == 1)
    def _():
        pl.semaphore_wait(pready, 1)
    exchange(z, core).start()
    for i in range(1, nz):
        @pl.when(z + i < nz)
        def _():
            pl.semaphore_wait(zready.at[i - 1], 1)
            send(z + i).start()
    exchange(z, 1 - core).wait_recv()
    for side, hold in enumerate(HOLDS):
        @pl.when((z > 1) & (core == side) & jnp.logical_not(relayed))
        def _():
            pl.delay(hold)
            for i in range(1, nz - 1):
                @pl.when(z > i)
                def _():
                    send(i).start()
    @pl.when(cd == 0)
    def _():
        pl.semaphore_wait(entered, cds - 1)
        for i in range(1, cds):
            signal(entered, "cd", i)

    load_a.wait()
    hi, lo = split(a[...])
    width = CORES * TILE
    for k in range(nz):
        c = slice(k * width, (k + 1) * width)
        a_cat[k] = jnp.concatenate([hi[:, c], lo[:, c], hi[:, c]], axis=1)

    def product(chip):
        stripes = []
        for i in range(CORES):
            t = tiles[chip * CORES + i]
            g = cd * pairs + chip * CORES + i
            stripes.append(jnp.concatenate(
                [t * flags[m, g].astype(jnp.float32) for m in range(blocks)], axis=1))
        b_hi, b_lo = split(jnp.concatenate(stripes, axis=0))
        return jnp.dot(
            a_cat[chip], jnp.concatenate([b_hi, b_hi, b_lo], axis=0), preferred_element_type=jnp.float32)

    def plain(j):
        return jnp.where(j <= z, z - j, j)

    def source(j):
        chip = plain(j)
        if nz > 3:
            chip = jnp.where((z == 0) & (j == 2), 3, jnp.where((z == 0) & (j == 3), 2, chip))
        return chip

    last = jnp.where(core == 0, source(nz - 1), plain(nz - 1))
    by_relay = (z == 0) & (core == 0) & (last == 2)

    def twice(chip):
        return (z == 0) & (core == 1) & (chip == 2)

    def receive(chip):
        arrival(chip).wait_recv()
        @pl.when((z == 1) & (core == 1) & (chip == 2))
        def _():
            for i in range(CORES):
                relay(i).start()
        @pl.when(jnp.logical_not(twice(chip)))
        def _():
            exchange(chip, core).start()

    def add(chip):
        exchange(chip, 1 - core).wait_recv()
        acc[...] += product(chip)

    acc[...] = product(z)

    def gather(j, carry):
        @pl.when(by_relay & (j == 2))
        def _():
            receive(last)
        receive(source(j))
        @pl.when(core == 0)
        def _():
            add(source(j))
        return carry

    def rest(j, carry):
        add(plain(j))
        return carry

    lax.fori_loop(1, nz - 1, gather, 0)
    @pl.when((core == 1) | jnp.logical_not(by_relay))
    def _():
        receive(source(nz - 1))
    @pl.when(core == 1)
    def _():
        lax.fori_loop(1, nz - 1, rest, 0)

    def scatter(q):
        return pltpu.make_async_remote_copy(
            src_ref=acc.at[pl.ds(q * rows, rows)], dst_ref=land.at[cd - jnp.where(cd > q, 1, 0)],
            send_sem=sem.at[2], recv_sem=rs_recv, device_id={"cd": q}, device_id_type=MESH)

    def scattered():
        return pltpu.make_async_remote_copy(
            src_ref=acc.at[pl.ds(0, (cds - 1) * rows)], dst_ref=land,
            send_sem=sem.at[2], recv_sem=rs_recv, device_id={"cd": lax.rem(cd + 1, cds)}, device_id_type=MESH)

    @pl.when(cd > 0)
    def _():
        pl.semaphore_wait(entered, 1)
    exchange(last, 1 - core).wait_recv()
    prod = product(last)
    for q in range(cds):
        r = slice(q * rows, (q + 1) * rows)
        acc[r] += prod[r]
        @pl.when(cd != q)
        def _():
            scatter(q).start()

    def drained(n, sem):
        return pltpu.make_async_remote_copy(
            src_ref=tiles.at[pl.ds(0, n)], dst_ref=tiles.at[pl.ds(0, n)], send_sem=sem, recv_sem=rsem.at[0],
            device_id={"pair": partner}, device_id_type=MESH)

    fewer = relayed | twice(2)
    @pl.when(jnp.logical_not(fewer))
    def _():
        drained(2 * nz - 1, sem.at[0]).wait_send()
    @pl.when(fewer)
    def _():
        drained(2 * nz - 2, sem.at[0]).wait_send()
    @pl.when((z == 1) & (core == 1))
    def _():
        drained(CORES, sem.at[1]).wait_send()

    total = acc[pl.ds(pl.multiple_of(cd * rows, rows), rows)]
    scattered().wait_recv()
    for i in range(cds - 1):
        total = total + land[i]
    out_ref[...] = total
    scattered().wait_send()


def solution(mesh):
    pairs, cds = mesh.shape["pair"], mesh.shape["cd"]
    nz = pairs // CORES

    def local(amplitudes, integrals, keep_tiles):
        n, depth = amplitudes.shape
        ab = integrals.shape[1]
        rows = n // cds
        return pl.pallas_call(
            functools.partial(kernel, pairs, cds),
            out_shape=pltpu.VMEM((rows, ab), jnp.float32),
            in_specs=[
                pl.BlockSpec(memory_space=pl.ANY),
                pl.BlockSpec(memory_space=pl.ANY),
                pl.BlockSpec(memory_space=pl.ANY),
            ],
            out_specs=pl.BlockSpec(memory_space=pltpu.VMEM),
            scratch_shapes=[
                pltpu.SMEM(keep_tiles.shape[::-1], jnp.int32),
                pltpu.VMEM(integrals.shape, jnp.float32),
                pltpu.VMEM((n, depth), jnp.float32),
                pltpu.VMEM((pairs, TILE, TILE), jnp.float32),
                pltpu.VMEM((nz, n, 3 * CORES * TILE), jnp.bfloat16),
                pltpu.VMEM((n, ab), jnp.float32),
                pltpu.VMEM((cds - 1, rows, ab), jnp.float32),
                pltpu.SemaphoreType.DMA((3,)),
                pltpu.SemaphoreType.DMA((nz - 1,)),
                pltpu.SemaphoreType.DMA((nz,)),
                pltpu.SemaphoreType.DMA,
                pltpu.SemaphoreType.REGULAR((nz - 1,)),
                pltpu.SemaphoreType.REGULAR,
                pltpu.SemaphoreType.REGULAR,
            ],
            compiler_params=pltpu.CompilerParams(collective_id=0, has_side_effects=True),
        )(keep_tiles.T, integrals, amplitudes)

    placed = (P("pair", "cd"), P(("cd", "pair"), None), P())
    return jax.shard_map(
        local, mesh=mesh, in_specs=placed, out_specs=P(("pair", "cd"), None), check_vma=False
    )
```

```python
import functools

import jax
import jax.numpy as jnp
from jax import lax
from jax.experimental import pallas as pl
from jax.experimental.pallas import tpu as pltpu
from jax.sharding import PartitionSpec as P

TILE = 128
CORES = 2
HOLDS = (1000, 700)
HOLD_SUMS = 600
MESH = pl.DeviceIdType.MESH


def split(x):
    hi = x.astype(jnp.bfloat16)
    lo = (x - hi.astype(jnp.float32)).astype(jnp.bfloat16)
    return hi, lo


def kernel(pairs, cds, flags_hbm, v_hbm, a_hbm, out_ref, flags, v, a, tiles, a_cat, acc, land,
           sem, rsem, precv, rs_recv, zready, pready, entered):
    nz = pairs // CORES
    me = lax.axis_index("pair")
    cd = lax.axis_index("cd")
    z = lax.div(me, CORES)
    core = lax.rem(me, CORES)
    partner = me + 1 - 2 * core
    blocks = v.shape[1] // TILE
    rows = out_ref.shape[0]

    load_v = pltpu.make_async_copy(v_hbm, v, sem.at[0])
    load_v.start()
    load_f = pltpu.make_async_copy(flags_hbm, flags, sem.at[2])
    load_f.start()
    load_a = pltpu.make_async_copy(a_hbm, a, sem.at[1])

    def signal(sem, axis, to):
        pl.semaphore_signal(sem, inc=1, device_id={axis: to}, device_id_type=MESH)

    barrier = pltpu.get_barrier_semaphore()
    for i in range(1, nz):
        @pl.when(z + i < nz)
        def _():
            signal(barrier, "pair", me + i * CORES)
    @pl.when(cd == 0)
    def _():
        for i in range(1, cds):
            signal(barrier, "cd", i)
    @pl.when(core == 1)
    def _():
        signal(barrier, "pair", partner)
    greeted = z + jnp.where(cd > 0, 1, 0) + 1 - core
    @pl.when(greeted > 0)
    def _():
        pl.semaphore_wait(barrier, greeted)
    for i in range(1, nz):
        @pl.when(z >= i)
        def _():
            signal(zready.at[i - 1], "pair", me - i * CORES)
    @pl.when(core == 0)
    def _():
        signal(pready, "pair", partner)
    @pl.when(cd > 0)
    def _():
        signal(entered, "cd", 0)

    load_f.wait()
    load_v.wait()
    row_block = cd * pairs + me
    own = v[:, :TILE] * flags[0, row_block].astype(jnp.float32)
    for m in range(1, blocks):
        own = own + v[:, m * TILE:(m + 1) * TILE] * flags[m, row_block].astype(jnp.float32)
    tiles[me] = own

    def send(chip):
        return pltpu.make_async_remote_copy(
            src_ref=tiles.at[me], dst_ref=tiles.at[me], send_sem=sem.at[0], recv_sem=rsem.at[z - jnp.where(z > chip, 1, 0)],
            device_id={"pair": chip * CORES + core}, device_id_type=MESH)

    def arrival(chip):
        k = chip * CORES + core
        return pltpu.make_async_remote_copy(
            src_ref=tiles.at[k], dst_ref=tiles.at[k], send_sem=sem.at[0], recv_sem=rsem.at[chip - jnp.where(chip > z, 1, 0)],
            device_id={"pair": k}, device_id_type=MESH)

    def relay(to):
        k = 2 * CORES + 1
        return pltpu.make_async_remote_copy(
            src_ref=tiles.at[k], dst_ref=tiles.at[k], send_sem=sem.at[1],
            recv_sem=rsem.at[1] if to else precv.at[2], device_id={"pair": to}, device_id_type=MESH)

    def exchange(chip, side):
        k = chip * CORES + side
        return pltpu.make_async_remote_copy(
            src_ref=tiles.at[k], dst_ref=tiles.at[k], send_sem=sem.at[0], recv_sem=precv.at[chip],
            device_id={"pair": partner}, device_id_type=MESH)

    relayed = (z == 2) & (core == 1)
    @pl.when(relayed)
    def _():
        send(1).start()
    @pl.when((z > 0) & jnp.logical_not(relayed))
    def _():
        send(0).start()
    load_a.start()
    @pl.when(core == 1)
    def _():
        pl.semaphore_wait(pready, 1)
    exchange(z, core).start()
    for i in range(1, nz):
        @pl.when(z + i < nz)
        def _():
            pl.semaphore_wait(zready.at[i - 1], 1)
            send(z + i).start()
    exchange(z, 1 - core).wait_recv()
    for side, hold in enumerate(HOLDS):
        @pl.when((z > 1) & (core == side) & jnp.logical_not(relayed))
        def _():
            pl.delay(hold)
            for i in range(1, nz - 1):
                @pl.when(z > i)
                def _():
                    send(i).start()
    @pl.when(cd == 0)
    def _():
        pl.semaphore_wait(entered, cds - 1)
        for i in range(1, cds):
            signal(entered, "cd", i)

    load_a.wait()
    hi, lo = split(a[...])
    width = CORES * TILE
    for k in range(nz):
        c = slice(k * width, (k + 1) * width)
        a_cat[k] = jnp.concatenate([hi[:, c], lo[:, c], hi[:, c]], axis=1)

    def product(chip):
        stripes = []
        for i in range(CORES):
            t = tiles[chip * CORES + i]
            g = cd * pairs + chip * CORES + i
            stripes.append(jnp.concatenate(
                [t * flags[m, g].astype(jnp.float32) for m in range(blocks)], axis=1))
        b_hi, b_lo = split(jnp.concatenate(stripes, axis=0))
        return jnp.dot(
            a_cat[chip], jnp.concatenate([b_hi, b_hi, b_lo], axis=0), preferred_element_type=jnp.float32)

    def plain(j):
        return jnp.where(j <= z, z - j, j)

    def source(j):
        chip = plain(j)
        if nz > 3:
            chip = jnp.where((z == 0) & (j == 2), 3, jnp.where((z == 0) & (j == 3), 2, chip))
        return chip

    last = jnp.where(core == 0, source(nz - 1), plain(nz - 1))
    by_relay = (z == 0) & (core == 0) & (last == 2)

    def twice(chip):
        return (z == 0) & (core == 1) & (chip == 2)

    def receive(chip):
        arrival(chip).wait_recv()
        @pl.when((z == 1) & (core == 1) & (chip == 2))
        def _():
            for i in range(CORES):
                relay(i).start()
        @pl.when(jnp.logical_not(twice(chip)))
        def _():
            exchange(chip, core).start()

    def add(chip):
        exchange(chip, 1 - core).wait_recv()
        acc[...] += product(chip)

    acc[...] = product(z)

    def gather(j, carry):
        @pl.when(by_relay & (j == 2))
        def _():
            receive(last)
        receive(source(j))
        @pl.when(core == 0)
        def _():
            add(source(j))
        return carry

    def rest(j, carry):
        add(plain(j))
        return carry

    lax.fori_loop(1, nz - 1, gather, 0)
    @pl.when((core == 1) | jnp.logical_not(by_relay))
    def _():
        receive(source(nz - 1))
    @pl.when(core == 1)
    def _():
        lax.fori_loop(1, nz - 1, rest, 0)

    def scatter(q):
        return pltpu.make_async_remote_copy(
            src_ref=acc.at[pl.ds(q * rows, rows)], dst_ref=land.at[cd - jnp.where(cd > q, 1, 0)],
            send_sem=sem.at[2], recv_sem=rs_recv, device_id={"cd": q}, device_id_type=MESH)

    def scattered():
        return pltpu.make_async_remote_copy(
            src_ref=acc.at[pl.ds(0, (cds - 1) * rows)], dst_ref=land,
            send_sem=sem.at[2], recv_sem=rs_recv, device_id={"cd": lax.rem(cd + 1, cds)}, device_id_type=MESH)

    @pl.when(cd > 0)
    def _():
        pl.semaphore_wait(entered, 1)
    exchange(last, 1 - core).wait_recv()
    prod = product(last)
    held = cd == 2
    for q in range(cds):
        r = slice(q * rows, (q + 1) * rows)
        acc[r] += prod[r]
        @pl.when((cd != q) & jnp.logical_not(held) if q == 1 else cd != q)
        def _():
            scatter(q).start()
    @pl.when(held)
    def _():
        pl.delay(HOLD_SUMS)
        scatter(1).start()

    def drained(n, sem):
        return pltpu.make_async_remote_copy(
            src_ref=tiles.at[pl.ds(0, n)], dst_ref=tiles.at[pl.ds(0, n)], send_sem=sem, recv_sem=rsem.at[0],
            device_id={"pair": partner}, device_id_type=MESH)

    fewer = relayed | twice(2)
    @pl.when(jnp.logical_not(fewer))
    def _():
        drained(2 * nz - 1, sem.at[0]).wait_send()
    @pl.when(fewer)
    def _():
        drained(2 * nz - 2, sem.at[0]).wait_send()
    @pl.when((z == 1) & (core == 1))
    def _():
        drained(CORES, sem.at[1]).wait_send()

    total = acc[pl.ds(pl.multiple_of(cd * rows, rows), rows)]
    scattered().wait_recv()
    for i in range(cds - 1):
        total = total + land[i]
    out_ref[...] = total
    scattered().wait_send()


def solution(mesh):
    pairs, cds = mesh.shape["pair"], mesh.shape["cd"]
    nz = pairs // CORES

    def local(amplitudes, integrals, keep_tiles):
        n, depth = amplitudes.shape
        ab = integrals.shape[1]
        rows = n // cds
        return pl.pallas_call(
            functools.partial(kernel, pairs, cds),
            out_shape=pltpu.VMEM((rows, ab), jnp.float32),
            in_specs=[
                pl.BlockSpec(memory_space=pl.ANY),
                pl.BlockSpec(memory_space=pl.ANY),
                pl.BlockSpec(memory_space=pl.ANY),
            ],
            out_specs=pl.BlockSpec(memory_space=pltpu.VMEM),
            scratch_shapes=[
                pltpu.SMEM(keep_tiles.shape[::-1], jnp.int32),
                pltpu.VMEM(integrals.shape, jnp.float32),
                pltpu.VMEM((n, depth), jnp.float32),
                pltpu.VMEM((pairs, TILE, TILE), jnp.float32),
                pltpu.VMEM((nz, n, 3 * CORES * TILE), jnp.bfloat16),
                pltpu.VMEM((n, ab), jnp.float32),
                pltpu.VMEM((cds - 1, rows, ab), jnp.float32),
                pltpu.SemaphoreType.DMA((3,)),
                pltpu.SemaphoreType.DMA((nz - 1,)),
                pltpu.SemaphoreType.DMA((nz,)),
                pltpu.SemaphoreType.DMA,
                pltpu.SemaphoreType.REGULAR((nz - 1,)),
                pltpu.SemaphoreType.REGULAR,
                pltpu.SemaphoreType.REGULAR,
            ],
            compiler_params=pltpu.CompilerParams(collective_id=0, has_side_effects=True),
        )(keep_tiles.T, integrals, amplitudes)

    placed = (P("pair", "cd"), P(("cd", "pair"), None), P())
    return jax.shard_map(
        local, mesh=mesh, in_specs=placed, out_specs=P(("pair", "cd"), None), check_vma=False
    )
```

```python
import functools

import jax
import jax.numpy as jnp
from jax import lax
from jax.experimental import pallas as pl
from jax.experimental.pallas import tpu as pltpu
from jax.sharding import PartitionSpec as P

TILE = 128
CORES = 2
HOLDS = (1000, 700)
HOLD_SUMS = 600
MESH = pl.DeviceIdType.MESH


def split(x):
    hi = x.astype(jnp.bfloat16)
    lo = (x - hi.astype(jnp.float32)).astype(jnp.bfloat16)
    return hi, lo


def kernel(pairs, cds, flags_hbm, v_hbm, a_hbm, out_ref, flags, v, a, tiles, a_cat, acc, land,
           sem, rsem, precv, rs_recv, zready, pready, entered):
    nz = pairs // CORES
    me = lax.axis_index("pair")
    cd = lax.axis_index("cd")
    z = lax.div(me, CORES)
    core = lax.rem(me, CORES)
    partner = me + 1 - 2 * core
    blocks = v.shape[1] // TILE
    rows = out_ref.shape[0]

    load_v = pltpu.make_async_copy(v_hbm, v, sem.at[0])
    load_v.start()
    load_f = pltpu.make_async_copy(flags_hbm, flags, sem.at[2])
    load_f.start()
    load_a = pltpu.make_async_copy(a_hbm, a, sem.at[1])

    def signal(sem, axis, to):
        pl.semaphore_signal(sem, inc=1, device_id={axis: to}, device_id_type=MESH)

    barrier = pltpu.get_barrier_semaphore()
    for i in range(1, nz):
        @pl.when(z + i < nz)
        def _():
            signal(barrier, "pair", me + i * CORES)
    @pl.when(cd == 0)
    def _():
        for i in range(1, cds):
            signal(barrier, "cd", i)
    @pl.when(core == 1)
    def _():
        signal(barrier, "pair", partner)
    greeted = z + jnp.where(cd > 0, 1, 0) + 1 - core
    @pl.when(greeted > 0)
    def _():
        pl.semaphore_wait(barrier, greeted)
    for i in range(1, nz):
        @pl.when(z >= i)
        def _():
            signal(zready.at[i - 1], "pair", me - i * CORES)
    @pl.when(core == 0)
    def _():
        signal(pready, "pair", partner)
    @pl.when(cd > 0)
    def _():
        signal(entered, "cd", 0)

    load_f.wait()
    load_v.wait()
    row_block = cd * pairs + me
    own = v[:, :TILE] * flags[0, row_block].astype(jnp.float32)
    for m in range(1, blocks):
        own = own + v[:, m * TILE:(m + 1) * TILE] * flags[m, row_block].astype(jnp.float32)
    tiles[me] = own

    def send(chip):
        return pltpu.make_async_remote_copy(
            src_ref=tiles.at[me], dst_ref=tiles.at[me], send_sem=sem.at[0], recv_sem=rsem.at[z - jnp.where(z > chip, 1, 0)],
            device_id={"pair": chip * CORES + core}, device_id_type=MESH)

    def arrival(chip):
        k = chip * CORES + core
        return pltpu.make_async_remote_copy(
            src_ref=tiles.at[k], dst_ref=tiles.at[k], send_sem=sem.at[0], recv_sem=rsem.at[chip - jnp.where(chip > z, 1, 0)],
            device_id={"pair": k}, device_id_type=MESH)

    def relay(to):
        k = 2 * CORES + 1
        return pltpu.make_async_remote_copy(
            src_ref=tiles.at[k], dst_ref=tiles.at[k], send_sem=sem.at[1],
            recv_sem=rsem.at[1] if to else precv.at[2], device_id={"pair": to}, device_id_type=MESH)

    def exchange(chip, side):
        k = chip * CORES + side
        return pltpu.make_async_remote_copy(
            src_ref=tiles.at[k], dst_ref=tiles.at[k], send_sem=sem.at[0], recv_sem=precv.at[chip],
            device_id={"pair": partner}, device_id_type=MESH)

    relayed = (z == 2) & (core == 1)
    @pl.when(relayed)
    def _():
        send(1).start()
    @pl.when((z > 0) & jnp.logical_not(relayed))
    def _():
        send(0).start()
    load_a.start()
    @pl.when(core == 1)
    def _():
        pl.semaphore_wait(pready, 1)
    exchange(z, core).start()
    for i in range(1, nz):
        @pl.when(z + i < nz)
        def _():
            pl.semaphore_wait(zready.at[i - 1], 1)
            send(z + i).start()
    exchange(z, 1 - core).wait_recv()
    for side, hold in enumerate(HOLDS):
        @pl.when((z > 1) & (core == side) & jnp.logical_not(relayed))
        def _():
            pl.delay(hold)
            for i in range(1, nz - 1):
                @pl.when(z > i)
                def _():
                    send(i).start()
    @pl.when(cd == 0)
    def _():
        pl.semaphore_wait(entered, cds - 1)
        for i in range(1, cds):
            signal(entered, "cd", i)

    load_a.wait()
    hi, lo = split(a[...])
    width = CORES * TILE
    for k in range(nz):
        c = slice(k * width, (k + 1) * width)
        a_cat[k] = jnp.concatenate([hi[:, c], lo[:, c], hi[:, c]], axis=1)

    def operands(chip, sides):
        stripes = []
        for i in sides:
            t = tiles[chip * CORES + i]
            g = cd * pairs + chip * CORES + i
            stripes.append(jnp.concatenate(
                [t * flags[m, g].astype(jnp.float32) for m in range(blocks)], axis=1))
        b_hi, b_lo = split(jnp.concatenate(stripes, axis=0))
        lo, hi = sides[0] * TILE, (sides[-1] + 1) * TILE
        left = [a_cat[chip, :, part * width + lo:part * width + hi] for part in range(3)]
        return left, [b_hi, b_hi, b_lo]

    def product(*terms):
        left, right = (sum(t, []) for t in zip(*(operands(*term) for term in terms)))
        return jnp.dot(
            jnp.concatenate(left, axis=1), jnp.concatenate(right, axis=0), preferred_element_type=jnp.float32)

    def plain(j):
        return jnp.where(j <= z, z - j, j)

    def source(j):
        chip = plain(j)
        if nz > 3:
            chip = jnp.where((z == 0) & (j == 2), 3, jnp.where((z == 0) & (j == 3), 2, chip))
        return chip

    last = jnp.where(core == 0, source(nz - 1), plain(nz - 1))
    by_relay = (z == 0) & (core == 0) & (last == 2)

    def twice(chip):
        return (z == 0) & (core == 1) & (chip == 2)

    def receive(chip):
        arrival(chip).wait_recv()
        @pl.when((z == 1) & (core == 1) & (chip == 2))
        def _():
            for i in range(CORES):
                relay(i).start()
        @pl.when(jnp.logical_not(twice(chip)))
        def _():
            exchange(chip, core).start()

    def add(chip):
        exchange(chip, 1 - core).wait_recv()
        acc[...] += product((chip, (0, 1)))

    acc[...] = product((z, (0, 1)))

    def gather(j, carry):
        @pl.when(by_relay & (j == 2))
        def _():
            receive(last)
        receive(source(j))
        @pl.when(core == 0)
        def _():
            add(source(j))
        return carry

    def rest(j, carry):
        add(plain(j))
        return carry

    lax.fori_loop(1, nz - 1, gather, 0)
    @pl.when((core == 1) | jnp.logical_not(by_relay))
    def _():
        receive(source(nz - 1))
    @pl.when(core == 1)
    def _():
        lax.fori_loop(1, nz - 2, rest, 0)
        before = plain(nz - 2)
        exchange(before, 0).wait_recv()
        acc[...] += product((before, (0, 1)), (last, (1,)))

    def scatter(q):
        return pltpu.make_async_remote_copy(
            src_ref=acc.at[pl.ds(q * rows, rows)], dst_ref=land.at[cd - jnp.where(cd > q, 1, 0)],
            send_sem=sem.at[2], recv_sem=rs_recv, device_id={"cd": q}, device_id_type=MESH)

    def scattered():
        return pltpu.make_async_remote_copy(
            src_ref=acc.at[pl.ds(0, (cds - 1) * rows)], dst_ref=land,
            send_sem=sem.at[2], recv_sem=rs_recv, device_id={"cd": lax.rem(cd + 1, cds)}, device_id_type=MESH)

    @pl.when(cd > 0)
    def _():
        pl.semaphore_wait(entered, 1)
    held = cd == 2

    def finish(prod):
        for q in range(cds):
            r = slice(q * rows, (q + 1) * rows)
            acc[r] += prod[r]
            @pl.when((cd != q) & jnp.logical_not(held) if q == 1 else cd != q)
            def _():
                scatter(q).start()

    exchange(last, 1 - core).wait_recv()
    for side, tail in enumerate(((0, 1), (0,))):
        @pl.when(core == side)
        def _():
            finish(product((last, tail)))
    @pl.when(held)
    def _():
        pl.delay(HOLD_SUMS)
        scatter(1).start()

    def drained(n, sem):
        return pltpu.make_async_remote_copy(
            src_ref=tiles.at[pl.ds(0, n)], dst_ref=tiles.at[pl.ds(0, n)], send_sem=sem, recv_sem=rsem.at[0],
            device_id={"pair": partner}, device_id_type=MESH)

    fewer = relayed | twice(2)
    @pl.when(jnp.logical_not(fewer))
    def _():
        drained(2 * nz - 1, sem.at[0]).wait_send()
    @pl.when(fewer)
    def _():
        drained(2 * nz - 2, sem.at[0]).wait_send()
    @pl.when((z == 1) & (core == 1))
    def _():
        drained(CORES, sem.at[1]).wait_send()

    total = acc[pl.ds(pl.multiple_of(cd * rows, rows), rows)]
    scattered().wait_recv()
    for i in range(cds - 1):
        total = total + land[i]
    out_ref[...] = total
    scattered().wait_send()


def solution(mesh):
    pairs, cds = mesh.shape["pair"], mesh.shape["cd"]
    nz = pairs // CORES

    def local(amplitudes, integrals, keep_tiles):
        n, depth = amplitudes.shape
        ab = integrals.shape[1]
        rows = n // cds
        return pl.pallas_call(
            functools.partial(kernel, pairs, cds),
            out_shape=pltpu.VMEM((rows, ab), jnp.float32),
            in_specs=[
                pl.BlockSpec(memory_space=pl.ANY),
                pl.BlockSpec(memory_space=pl.ANY),
                pl.BlockSpec(memory_space=pl.ANY),
            ],
            out_specs=pl.BlockSpec(memory_space=pltpu.VMEM),
            scratch_shapes=[
                pltpu.SMEM(keep_tiles.shape[::-1], jnp.int32),
                pltpu.VMEM(integrals.shape, jnp.float32),
                pltpu.VMEM((n, depth), jnp.float32),
                pltpu.VMEM((pairs, TILE, TILE), jnp.float32),
                pltpu.VMEM((nz, n, 3 * CORES * TILE), jnp.bfloat16),
                pltpu.VMEM((n, ab), jnp.float32),
                pltpu.VMEM((cds - 1, rows, ab), jnp.float32),
                pltpu.SemaphoreType.DMA((3,)),
                pltpu.SemaphoreType.DMA((nz - 1,)),
                pltpu.SemaphoreType.DMA((nz,)),
                pltpu.SemaphoreType.DMA,
                pltpu.SemaphoreType.REGULAR((nz - 1,)),
                pltpu.SemaphoreType.REGULAR,
                pltpu.SemaphoreType.REGULAR,
            ],
            compiler_params=pltpu.CompilerParams(collective_id=0, has_side_effects=True),
        )(keep_tiles.T, integrals, amplitudes)

    placed = (P("pair", "cd"), P(("cd", "pair"), None), P())
    return jax.shard_map(
        local, mesh=mesh, in_specs=placed, out_specs=P(("pair", "cd"), None), check_vma=False
    )
```

```python
import functools

import jax
import jax.numpy as jnp
from jax import lax
from jax.experimental import pallas as pl
from jax.experimental.pallas import tpu as pltpu
from jax.sharding import PartitionSpec as P

TILE = 128
CORES = 2
HOLDS = (950, 600)
HOLD_SUMS = 450
MESH = pl.DeviceIdType.MESH


def split(x):
    hi = x.astype(jnp.bfloat16)
    lo = (x - hi.astype(jnp.float32)).astype(jnp.bfloat16)
    return hi, lo


def kernel(pairs, cds, flags_hbm, v_hbm, a_hbm, out_ref, flags, v, a, tiles, a_cat, acc, land,
           sem, rsem, precv, rs_recv, zready, pready, entered):
    nz = pairs // CORES
    me = lax.axis_index("pair")
    cd = lax.axis_index("cd")
    z = lax.div(me, CORES)
    core = lax.rem(me, CORES)
    partner = me + 1 - 2 * core
    blocks = v.shape[1] // TILE
    rows = out_ref.shape[0]

    load_v = pltpu.make_async_copy(v_hbm, v, sem.at[0])
    load_v.start()
    load_f = pltpu.make_async_copy(flags_hbm, flags, sem.at[2])
    load_f.start()
    load_a = pltpu.make_async_copy(a_hbm, a, sem.at[1])

    def signal(sem, axis, to):
        pl.semaphore_signal(sem, inc=1, device_id={axis: to}, device_id_type=MESH)

    barrier = pltpu.get_barrier_semaphore()
    for i in range(1, nz):
        @pl.when(z + i < nz)
        def _():
            signal(barrier, "pair", me + i * CORES)
    @pl.when(cd == 0)
    def _():
        for i in range(1, cds):
            signal(barrier, "cd", i)
    @pl.when(core == 1)
    def _():
        signal(barrier, "pair", partner)
    greeted = z + jnp.where(cd > 0, 1, 0) + 1 - core
    @pl.when(greeted > 0)
    def _():
        pl.semaphore_wait(barrier, greeted)
    for i in range(1, nz):
        @pl.when(z >= i)
        def _():
            signal(zready.at[i - 1], "pair", me - i * CORES)
    @pl.when(core == 0)
    def _():
        signal(pready, "pair", partner)
    @pl.when(cd > 0)
    def _():
        signal(entered, "cd", 0)

    load_f.wait()
    load_v.wait()
    row_block = cd * pairs + me
    own = v[:, :TILE] * flags[0, row_block].astype(jnp.float32)
    for m in range(1, blocks):
        own = own + v[:, m * TILE:(m + 1) * TILE] * flags[m, row_block].astype(jnp.float32)
    tiles[me] = own

    def send(chip):
        return pltpu.make_async_remote_copy(
            src_ref=tiles.at[me], dst_ref=tiles.at[me], send_sem=sem.at[0], recv_sem=rsem.at[z - jnp.where(z > chip, 1, 0)],
            device_id={"pair": chip * CORES + core}, device_id_type=MESH)

    def arrival(chip):
        k = chip * CORES + core
        return pltpu.make_async_remote_copy(
            src_ref=tiles.at[k], dst_ref=tiles.at[k], send_sem=sem.at[0], recv_sem=rsem.at[chip - jnp.where(chip > z, 1, 0)],
            device_id={"pair": k}, device_id_type=MESH)

    def relay(to):
        k = 2 * CORES + 1
        return pltpu.make_async_remote_copy(
            src_ref=tiles.at[k], dst_ref=tiles.at[k], send_sem=sem.at[1],
            recv_sem=rsem.at[1] if to else precv.at[2], device_id={"pair": to}, device_id_type=MESH)

    def exchange(chip, side):
        k = chip * CORES + side
        return pltpu.make_async_remote_copy(
            src_ref=tiles.at[k], dst_ref=tiles.at[k], send_sem=sem.at[0], recv_sem=precv.at[chip],
            device_id={"pair": partner}, device_id_type=MESH)

    relayed = (z == 2) & (core == 1)
    @pl.when(relayed)
    def _():
        send(1).start()
    @pl.when((z > 0) & jnp.logical_not(relayed))
    def _():
        send(0).start()
    load_a.start()
    @pl.when(core == 1)
    def _():
        pl.semaphore_wait(pready, 1)
    exchange(z, core).start()
    for i in range(1, nz):
        @pl.when(z + i < nz)
        def _():
            pl.semaphore_wait(zready.at[i - 1], 1)
            send(z + i).start()
    exchange(z, 1 - core).wait_recv()
    for side, hold in enumerate(HOLDS):
        @pl.when((z > 1) & (core == side) & jnp.logical_not(relayed))
        def _():
            pl.delay(hold)
            for i in range(1, nz - 1):
                @pl.when(z > i)
                def _():
                    send(i).start()
    @pl.when(cd == 0)
    def _():
        pl.semaphore_wait(entered, cds - 1)
        for i in range(1, cds):
            signal(entered, "cd", i)

    load_a.wait()
    hi, lo = split(a[...])
    width = CORES * TILE
    for k in range(nz):
        c = slice(k * width, (k + 1) * width)
        a_cat[k] = jnp.concatenate([hi[:, c], lo[:, c], hi[:, c]], axis=1)

    def product(chip):
        stripes = []
        for i in range(CORES):
            t = tiles[chip * CORES + i]
            g = cd * pairs + chip * CORES + i
            stripes.append(jnp.concatenate(
                [t * flags[m, g].astype(jnp.float32) for m in range(blocks)], axis=1))
        b_hi, b_lo = split(jnp.concatenate(stripes, axis=0))
        return jnp.dot(
            a_cat[chip], jnp.concatenate([b_hi, b_hi, b_lo], axis=0), preferred_element_type=jnp.float32)

    def plain(j):
        return jnp.where(j <= z, z - j, j)

    def source(j):
        chip = plain(j)
        if nz > 3:
            chip = jnp.where((z == 0) & (j == 2), 3, jnp.where((z == 0) & (j == 3), 2, chip))
        return chip

    last = jnp.where(core == 0, source(nz - 1), plain(nz - 1))
    by_relay = (z == 0) & (core == 0) & (last == 2)

    def twice(chip):
        return (z == 0) & (core == 1) & (chip == 2)

    def receive(chip):
        arrival(chip).wait_recv()
        @pl.when((z == 1) & (core == 1) & (chip == 2))
        def _():
            for i in range(CORES):
                relay(i).start()
        @pl.when(jnp.logical_not(twice(chip)))
        def _():
            exchange(chip, core).start()

    def add(chip):
        exchange(chip, 1 - core).wait_recv()
        acc[...] += product(chip)

    acc[...] = product(z)

    def gather(j, carry):
        @pl.when(by_relay & (j == 2))
        def _():
            receive(last)
        receive(source(j))
        @pl.when(core == 0)
        def _():
            add(source(j))
        return carry

    def rest(j, carry):
        add(plain(j))
        return carry

    lax.fori_loop(1, nz - 1, gather, 0)
    @pl.when((core == 1) | jnp.logical_not(by_relay))
    def _():
        receive(source(nz - 1))
    @pl.when(core == 1)
    def _():
        lax.fori_loop(1, nz - 1, rest, 0)

    def scatter(q):
        return pltpu.make_async_remote_copy(
            src_ref=acc.at[pl.ds(q * rows, rows)], dst_ref=land.at[cd - jnp.where(cd > q, 1, 0)],
            send_sem=sem.at[2], recv_sem=rs_recv, device_id={"cd": q}, device_id_type=MESH)

    def scattered():
        return pltpu.make_async_remote_copy(
            src_ref=acc.at[pl.ds(0, (cds - 1) * rows)], dst_ref=land,
            send_sem=sem.at[2], recv_sem=rs_recv, device_id={"cd": lax.rem(cd + 1, cds)}, device_id_type=MESH)

    @pl.when(cd > 0)
    def _():
        pl.semaphore_wait(entered, 1)
    exchange(last, 1 - core).wait_recv()
    prod = product(last)
    held = cd == 2
    for q in range(cds):
        r = slice(q * rows, (q + 1) * rows)
        acc[r] += prod[r]
        @pl.when((cd != q) & jnp.logical_not(held) if q == 1 else cd != q)
        def _():
            scatter(q).start()
    @pl.when(held)
    def _():
        pl.delay(HOLD_SUMS)
        scatter(1).start()

    def drained(n, sem):
        return pltpu.make_async_remote_copy(
            src_ref=tiles.at[pl.ds(0, n)], dst_ref=tiles.at[pl.ds(0, n)], send_sem=sem, recv_sem=rsem.at[0],
            device_id={"pair": partner}, device_id_type=MESH)

    fewer = relayed | twice(2)
    @pl.when(jnp.logical_not(fewer))
    def _():
        drained(2 * nz - 1, sem.at[0]).wait_send()
    @pl.when(fewer)
    def _():
        drained(2 * nz - 2, sem.at[0]).wait_send()
    @pl.when((z == 1) & (core == 1))
    def _():
        drained(CORES, sem.at[1]).wait_send()

    total = acc[pl.ds(pl.multiple_of(cd * rows, rows), rows)]
    scattered().wait_recv()
    for i in range(cds - 1):
        total = total + land[i]
    out_ref[...] = total
    scattered().wait_send()


def solution(mesh):
    pairs, cds = mesh.shape["pair"], mesh.shape["cd"]
    nz = pairs // CORES

    def local(amplitudes, integrals, keep_tiles):
        n, depth = amplitudes.shape
        ab = integrals.shape[1]
        rows = n // cds
        return pl.pallas_call(
            functools.partial(kernel, pairs, cds),
            out_shape=pltpu.VMEM((rows, ab), jnp.float32),
            in_specs=[
                pl.BlockSpec(memory_space=pl.ANY),
                pl.BlockSpec(memory_space=pl.ANY),
                pl.BlockSpec(memory_space=pl.ANY),
            ],
            out_specs=pl.BlockSpec(memory_space=pltpu.VMEM),
            scratch_shapes=[
                pltpu.SMEM(keep_tiles.shape[::-1], jnp.int32),
                pltpu.VMEM(integrals.shape, jnp.float32),
                pltpu.VMEM((n, depth), jnp.float32),
                pltpu.VMEM((pairs, TILE, TILE), jnp.float32),
                pltpu.VMEM((nz, n, 3 * CORES * TILE), jnp.bfloat16),
                pltpu.VMEM((n, ab), jnp.float32),
                pltpu.VMEM((cds - 1, rows, ab), jnp.float32),
                pltpu.SemaphoreType.DMA((3,)),
                pltpu.SemaphoreType.DMA((nz - 1,)),
                pltpu.SemaphoreType.DMA((nz,)),
                pltpu.SemaphoreType.DMA,
                pltpu.SemaphoreType.REGULAR((nz - 1,)),
                pltpu.SemaphoreType.REGULAR,
                pltpu.SemaphoreType.REGULAR,
            ],
            compiler_params=pltpu.CompilerParams(collective_id=0, has_side_effects=True),
        )(keep_tiles.T, integrals, amplitudes)

    placed = (P("pair", "cd"), P(("cd", "pair"), None), P())
    return jax.shard_map(
        local, mesh=mesh, in_specs=placed, out_specs=P(("pair", "cd"), None), check_vma=False
    )
```
